32 devices in a mesh: dp: 4 (over z), member: 2 (over x), space: 4 (over y, core).
Axes of the slice: x: 2, y: 2, z: 4, core: 2. Of those that a mesh axis runs over, the one named last changes fastest.
Arguments:
- grid_in: bfloat16 [4, 84, 2048], P('dp', None, 'space'), may hold values from -6 to 6
- target: bfloat16 [4, 84, 2048], P('dp', None, 'space'), may hold values from -6 to 6
- noise: float32 [4, 8, 32], P('dp', 'member'), may hold values from -6 to 6
- neighbours: int32 [8, 3], P('space'), may hold values from 0 to 7, as said below
- enc_index: int32 [512, 4], P('space'), may hold values from 0 to 2047, as said below
- dec_index: int32 [2048, 3], P('space'), may hold values from 0 to 511, as said below
- w_in: bfloat16 [84, 768], replicated, may hold values from -0.625 to 0.625
- w_gamma: float32 [32, 768], replicated, may hold values from -0.6 to 0.6
- w_beta: float32 [32, 768], replicated, may hold values from -0.6 to 0.6
- w_qkv: bfloat16 [768, 2304], replicated, may hold values from -60 to 60
- w_o: bfloat16 [768, 768], replicated, may hold values from -0.8984375 to 0.8984375
- readout_matrix: bfloat16 [84, 768], replicated, may hold values from -0.21875 to 0.21875
Outputs:
- predicted_states: bfloat16 [4, 8, 84, 2048], P('dp', 'member', None, 'space')
- objective_mean: float32 [], replicated
- unit_descent_slope: float32 [84, 768], replicated
The draws below stay inside these ranges and needn't reach their ends.
Inputs may be any that keep to these rules, and one draw needn't show every extreme that they name: `neighbours`: row w lists three different windows other than w whose ids differ from w by 1 or 2, counted around the 8 windows. `enc_index`: rows j * 128 to (j + 1) * 128 - 1 name only grid points j * 512 to (j + 1) * 512 - 1. `dec_index`: rows j * 512 to (j + 1) * 512 - 1 name only tokens j * 128 to (j + 1) * 128 - 1.
All inputs are finite; a program needn't handle non-finite values.
Results may differ from the reference program's by a relative error of at most 0.0065.
The reference program's roundings to bfloat16 on the way count: a program that leaves them out, or rounds other values in their place, can miss the bound.
Values may be sent and summed in bfloat16 or wider, within the bound.
A program may use at most 128 MiB of HBM per device.

```python
import jax
import jax.numpy as jnp
from jax import lax

V = 84
D = 768
HEADS = 12
HD = 64
NZ = 32
WIN = 64
NBR = 3
K_ENC = 4
K_DEC = 3
TOK_DEV = 128
G_DEV = 512
SAMPLES = 4
MEMBERS = 8
TOKENS = 512
GRID = 2048
N_SPACE = 4


def draw_neighbours(key, part):
    total = TOK_DEV // WIN * N_SPACE
    shifts = jnp.array([-2, -1, 1, 2], dtype=jnp.int32)
    dropped = jax.random.randint(jax.random.fold_in(key, 11), (total, 1), 0, 4)
    slots = jnp.arange(3, dtype=jnp.int32)[None, :]
    picked = slots + (slots >= dropped).astype(jnp.int32)
    return ((jnp.arange(total, dtype=jnp.int32)[:, None] + shifts[picked]) % total).astype(jnp.int32)


def draw_enc_index(key, part):
    rows = TOK_DEV * N_SPACE
    blocks = jnp.arange(rows, dtype=jnp.int32) // TOK_DEV
    offsets = jax.random.randint(jax.random.fold_in(key, 23), (rows, K_ENC), 0, G_DEV)
    return (blocks[:, None] * G_DEV + offsets).astype(jnp.int32)


def draw_dec_index(key, part):
    rows = G_DEV * N_SPACE
    blocks = jnp.arange(rows, dtype=jnp.int32) // G_DEV
    offsets = jax.random.randint(jax.random.fold_in(key, 37), (rows, K_DEC), 0, TOK_DEV)
    return (blocks[:, None] * TOK_DEV + offsets).astype(jnp.int32)


def draw_w_qkv(key, part):
    base = jax.random.normal(jax.random.fold_in(key, 41), (D, 3 * D), jnp.float32)
    base = jnp.clip(base, -6.0, 6.0) / jnp.sqrt(jnp.float32(D))
    return base.astype(jnp.bfloat16)


def shard_levels(own_key, extent, cuts, smallest, high):
    def one(dim, parts):
        draws = jax.random.uniform(jax.random.fold_in(jax.random.fold_in(own_key, 6), dim), (parts,), jnp.float32, smallest / len(cuts), high / len(cuts))
        return jnp.repeat(jnp.exp(draws), extent[dim] // parts).reshape((-1,) + (1,) * (len(extent) - dim - 1))

    gain = one(*cuts[0])
    for cut in cuts[1:]:
        gain = gain * one(*cut)
    return gain


def normal_values(stream_key, shape, deviation, limit, split=(), held_as=jnp.bfloat16):
    values = jax.random.normal(stream_key, shape, jnp.float32) * deviation
    if len(split) > 0:
        values = shard_levels(stream_key, shape, split, -0.22, 0.18) * values
    return jnp.clip(values, min=-limit, max=limit).astype(held_as)


def setup_inputs(seed: int = 0) -> dict:
    arg_keys = jax.random.split(jax.random.key(seed), 13)
    return {
        "grid_in": normal_values(arg_keys[0], (SAMPLES, V, GRID), 1.0, 6.0, ((0, 4), (2, 4))),
        "target": normal_values(arg_keys[1], (SAMPLES, V, GRID), 1.0, 6.0, ((0, 4), (2, 4))),
        "noise": normal_values(arg_keys[2], (SAMPLES, MEMBERS, NZ), 1.0, 6.0, ((0, 4), (1, 2)), jnp.float32),
        "neighbours": draw_neighbours(jax.random.fold_in(arg_keys[12], 71), 0),
        "enc_index": draw_enc_index(jax.random.fold_in(arg_keys[12], 71), 0),
        "dec_index": draw_dec_index(jax.random.fold_in(arg_keys[12], 71), 0),
        "w_in": normal_values(arg_keys[6], (V, D), V ** -0.5, 0.625),
        "w_gamma": normal_values(arg_keys[7], (NZ, D), 0.1, 0.6, (), jnp.float32),
        "w_beta": normal_values(arg_keys[8], (NZ, D), 0.1, 0.6, (), jnp.float32),
        "w_qkv": draw_w_qkv(jax.random.fold_in(arg_keys[12], 71), 0),
        "w_o": normal_values(arg_keys[10], (D, D), 0.15, 0.8984375),
        "readout_matrix": normal_values(arg_keys[11], (V, D), D ** -0.5, 0.21875),
    }


EPSILON = 1e-06

def layer_norm(values):
    centre = values - lax.optimization_barrier(jnp.mean(values, axis=-1, keepdims=True))
    spread = lax.optimization_barrier(jnp.mean(centre * centre, axis=-1, keepdims=True))
    return centre / jnp.sqrt(spread + EPSILON)

def conditioning(noise_rows, w_gamma, w_beta):
    scaling_factors = 1.0 + jnp.dot(noise_rows, w_gamma, precision=lax.Precision.HIGHEST)
    shift_terms_list = jnp.dot(noise_rows, w_beta, precision=lax.Precision.HIGHEST)
    return (scaling_factors, shift_terms_list)

def reference(grid_in, target, noise, neighbours, enc_index, dec_index, w_in, w_gamma, w_beta, w_qkv, w_o, readout_matrix):
    windows = TOKENS // WIN
    window_order = jnp.concatenate([jnp.arange(windows, dtype=jnp.int32)[:, None], neighbours.astype(jnp.int32)], axis=1)
    score_scale = HD ** (-0.5)
    pair_mask = 1.0 - jnp.eye(MEMBERS, dtype=jnp.float32)
    score_sum = jnp.zeros((), jnp.float32)
    gradient = jnp.zeros((V, D), jnp.float32)
    prediction_results = []
    for sample in range(SAMPLES):
        predicted_quantities = grid_in[sample]
        embedded = jnp.dot(predicted_quantities.T, w_in, preferred_element_type=jnp.float32)
        states = embedded[enc_index[:, 0]]
        for column in range(1, K_ENC):
            states = states + embedded[enc_index[:, column]]
        states = states / K_ENC
        normed = layer_norm(states)
        scaling_factors, shift_terms_list = conditioning(noise[sample], w_gamma, w_beta)

        def realization_sweep(conditions):
            gain_one, bias_one = conditions
            inputs = (normed * gain_one + bias_one).astype(jnp.bfloat16)
            project = jnp.dot(inputs, w_qkv, preferred_element_type=jnp.float32).astype(jnp.bfloat16)
            queries = project[:, :D].reshape(windows, WIN, HEADS, HD).astype(jnp.float32)
            key_rows = project[:, D:2 * D].reshape(windows, WIN, HEADS, HD)[window_order]
            key_rows = key_rows.reshape(windows, (1 + NBR) * WIN, HEADS, HD).astype(jnp.float32)
            value_rows = project[:, 2 * D:].reshape(windows, WIN, HEADS, HD)[window_order]
            value_rows = value_rows.reshape(windows, (1 + NBR) * WIN, HEADS, HD).astype(jnp.float32)
            scores = jnp.einsum('wqhd,wkhd->whqk', queries, key_rows) * score_scale
            weights = lax.optimization_barrier(jax.nn.softmax(scores, axis=-1).astype(jnp.bfloat16))
            attended = jnp.einsum('whqk,wkhd->wqhd', weights.astype(jnp.float32), value_rows)
            attended = attended.astype(jnp.bfloat16).reshape(TOKENS, D)
            updated = states + jnp.dot(attended, w_o, preferred_element_type=jnp.float32)
            gathered = updated[dec_index[:, 0]]
            for column in range(1, K_DEC):
                gathered = gathered + updated[dec_index[:, column]]
            hidden_activations = (gathered / K_DEC).astype(jnp.bfloat16)
            predicted_states = (predicted_quantities.astype(jnp.float32) + jnp.dot(readout_matrix, hidden_activations.T, preferred_element_type=jnp.float32)).astype(jnp.bfloat16)
            return (predicted_states, hidden_activations)
        realization_prediction, realization_hidden = lax.map(realization_sweep, (scaling_factors, shift_terms_list))
        prediction_results.append(realization_prediction)
        complete_quantities = realization_prediction.astype(jnp.float32)
        truth = target[sample].astype(jnp.float32)
        to_truth = jnp.sqrt(lax.optimization_barrier(jnp.sum((complete_quantities - truth) ** 2, axis=(1, 2))) + EPSILON)

        def pair_row(other_row):
            return lax.optimization_barrier(jnp.sum((other_row - complete_quantities) ** 2, axis=(1, 2)))
        pair_dist = jnp.sqrt(lax.map(pair_row, complete_quantities) + EPSILON)
        sample_score = jnp.sum(to_truth) / MEMBERS - jnp.sum(pair_dist * pair_mask) / (2.0 * MEMBERS * MEMBERS)
        score_sum = score_sum + sample_score
        truth_pull = 1.0 / (MEMBERS * to_truth)
        pair_pull = pair_mask / (MEMBERS * MEMBERS * pair_dist)
        slope_bf = (truth_pull[:, None, None] * (complete_quantities - truth) - lax.optimization_barrier(jnp.sum(pair_pull, axis=1))[:, None, None] * complete_quantities + jnp.einsum('mn,nvg->mvg', pair_pull, complete_quantities, precision=lax.Precision.HIGHEST)).astype(jnp.bfloat16)
        for member_index in range(MEMBERS):
            gradient = gradient + jnp.dot(slope_bf[member_index], realization_hidden[member_index], preferred_element_type=jnp.float32)
    prediction_per_realization = jnp.stack(prediction_results, axis=0)
    objective_mean = score_sum / (SAMPLES * jnp.sqrt(jnp.float32(V * GRID)))
    unit_descent_slope = gradient / jnp.sqrt(jnp.mean(gradient * gradient) + EPSILON)
    return (prediction_per_realization, objective_mean, unit_descent_slope)
```

```python
import functools

import jax
import jax.numpy as jnp
from jax import lax
from jax.experimental import pallas as pl
from jax.experimental.pallas import tpu as pltpu
from jax.sharding import PartitionSpec as P

HEADS = 12
HD = 64
WIN = 64
EPSILON = 1e-06
F32 = jnp.float32
BF16 = jnp.bfloat16
NT = (((1,), (1,)), ((), ()))
VMEM_LIMIT = 60000 * 1024


def parts(values):
    hi = values.astype(BF16)
    rest = values - hi.astype(F32)
    mid = rest.astype(BF16)
    lo = (rest - mid.astype(F32)).astype(BF16)
    return hi, mid, lo


def counts_of(index, targets):
    positions = lax.broadcasted_iota(jnp.int32, (index.shape[0], targets), 1)
    counts = jnp.zeros((index.shape[0], targets), F32)
    for column in range(index.shape[1]):
        counts = counts + jnp.where(index[:, column : column + 1] == positions, 1.0, 0.0)
    return counts.astype(BF16)


def member_kernel(
    reach_ref, grid_ref, enc_ref, dec_ref, noise_ref, w_in_ref, w_gamma_ref, w_beta_ref,
    w_qkv_ref, w_o_ref, readout_ref,
    pred_ref, feat_ref,
    states_ref, normed_ref, gain_ref, shift_ref, dec_counts_ref, bias_ref, q_ref, kv_ref, att_ref,
):
    m = pl.program_id(0)
    tok = enc_ref.shape[1]
    grid_dev = grid_ref.shape[2]
    d_model = w_o_ref.shape[0]
    k_enc = enc_ref.shape[2]
    k_dec = dec_ref.shape[1]
    windows = tok // WIN

    @pl.when(m == 0)
    def _():
        for block in range(3):
            counts = counts_of(enc_ref[block], grid_dev)
            pooled = lax.dot_general(counts, grid_ref[block], NT, preferred_element_type=F32)
            states = jnp.zeros((tok, d_model), F32)
            for part in parts(pooled):
                states = states + jnp.dot(part, w_in_ref[...], preferred_element_type=F32)
            states = states * (1.0 / k_enc)
            if block == 0:
                states_ref[...] = states
            centre = states - jnp.mean(states, axis=-1, keepdims=True)
            spread = jnp.mean(centre * centre, axis=-1, keepdims=True)
            normed_ref[block * tok : (block + 1) * tok, :] = centre / jnp.sqrt(spread + EPSILON)
        noise = noise_ref[...]
        gain_ref[...] = 1.0 + jnp.dot(
            noise, w_gamma_ref[...], precision=lax.Precision.HIGHEST, preferred_element_type=F32
        )
        shift_ref[...] = jnp.dot(
            noise, w_beta_ref[...], precision=lax.Precision.HIGHEST, preferred_element_type=F32
        )
        dec_counts_ref[...] = counts_of(dec_ref[...], tok)
        lane = lax.broadcasted_iota(jnp.int32, (WIN, 3 * tok), 1)
        for window in range(windows):
            lo = window * WIN
            open_keys = (lane >= lo) & (lane < lo + WIN)
            for slot in range(reach_ref.shape[1]):
                start = reach_ref[window, slot]
                open_keys = open_keys | ((lane >= start) & (lane < start + WIN))
            row = jnp.where(open_keys, 0.0, -jnp.inf).astype(F32)
            bias_ref[lo : lo + WIN, :] = row
            bias_ref[tok + lo : tok + lo + WIN, :] = row

    inputs = (normed_ref[...] * gain_ref[pl.ds(m, 1), :] + shift_ref[pl.ds(m, 1), :]).astype(BF16)
    q_ref[...] = jnp.dot(
        inputs[:tok], w_qkv_ref[:, :d_model], preferred_element_type=F32
    ).astype(BF16)
    kv_ref[...] = jnp.dot(
        inputs, w_qkv_ref[:, d_model:], preferred_element_type=F32
    ).astype(BF16)
    pair_lane = lax.broadcasted_iota(jnp.int32, (tok, 2 * HD), 1)
    first = jnp.where(pair_lane < HD, HD ** (-0.5), 0.0).astype(BF16)
    second = jnp.where(pair_lane < HD, 0.0, HD ** (-0.5)).astype(BF16)
    for pair in range(d_model // (2 * HD)):
        cols = slice(pair * 2 * HD, (pair + 1) * 2 * HD)
        q = q_ref[:, cols]
        both = jnp.concatenate([q * first, q * second], axis=0)
        scores = lax.dot_general(both, kv_ref[:, cols], NT, preferred_element_type=F32)
        scores = scores + bias_ref[...]
        e = jnp.exp(scores - jnp.max(scores, axis=-1, keepdims=True))
        weights = (e * (1.0 / jnp.sum(e, axis=-1, keepdims=True))).astype(BF16)
        v = kv_ref[:, d_model + pair * 2 * HD : d_model + (pair + 1) * 2 * HD]
        out = jnp.dot(weights, v, preferred_element_type=F32)
        att_ref[:, cols] = jnp.where(pair_lane < HD, out[:tok], out[tok:]).astype(BF16)
    updated = states_ref[...] + jnp.dot(att_ref[...], w_o_ref[...], preferred_element_type=F32)
    dec_counts = dec_counts_ref[...]
    features = (
        jnp.dot(
            jnp.concatenate([dec_counts] * 3, axis=1),
            jnp.concatenate(parts(updated), axis=0),
            preferred_element_type=F32,
        )
        * (1.0 / k_dec)
    ).astype(BF16)
    feat_ref[0] = features
    pred_ref[0] = (
        grid_ref[0].astype(F32)
        + lax.dot_general(readout_ref[...], features, NT, preferred_element_type=F32)
    ).astype(BF16)


def forecasts(reach, grid3, enc3, dec_local, noise, w_in, w_gamma, w_beta, w_qkv, w_o, readout):
    members = noise.shape[0]
    tok = enc3.shape[1]
    v_count, grid_dev = grid3.shape[1:]
    d_model = w_o.shape[0]
    whole = pl.BlockSpec(memory_space=pltpu.VMEM)
    return pl.pallas_call(
        member_kernel,
        grid=(members,),
        out_shape=(
            jax.ShapeDtypeStruct((members, v_count, grid_dev), BF16),
            jax.ShapeDtypeStruct((members, grid_dev, d_model), BF16),
        ),
        in_specs=[pl.BlockSpec(memory_space=pltpu.SMEM)] + [whole] * 10,
        out_specs=(
            pl.BlockSpec((1, v_count, grid_dev), lambda m: (m, 0, 0)),
            pl.BlockSpec((1, grid_dev, d_model), lambda m: (m, 0, 0)),
        ),
        scratch_shapes=[
            pltpu.VMEM((tok, d_model), F32),
            pltpu.VMEM((3 * tok, d_model), F32),
            pltpu.VMEM((members, d_model), F32),
            pltpu.VMEM((members, d_model), F32),
            pltpu.VMEM((grid_dev, tok), BF16),
            pltpu.VMEM((2 * tok, 3 * tok), F32),
            pltpu.VMEM((tok, d_model), BF16),
            pltpu.VMEM((3 * tok, 2 * d_model), BF16),
            pltpu.VMEM((tok, d_model), BF16),
        ],
        compiler_params=pltpu.CompilerParams(vmem_limit_bytes=VMEM_LIMIT),
        name="forecasts",
    )(reach, grid3, enc3, dec_local, noise, w_in, w_gamma, w_beta, w_qkv, w_o, readout)


def shifted(values, step):
    count = lax.axis_size("space")
    return lax.ppermute(values, "space", [(i, (i + step) % count) for i in range(count)])


def front(grid_in, noise, neighbours, enc_index, dec_index, w_in, w_gamma, w_beta, w_qkv, w_o, readout):
    tok = enc_index.shape[0]
    grid_dev = dec_index.shape[0]
    block = lax.axis_index("space")
    enc_local = enc_index - block * grid_dev
    dec_local = dec_index - block * tok
    grid3 = jnp.stack([grid_in, shifted(grid_in, 1), shifted(grid_in, -1)])
    enc3 = jnp.stack([enc_local, shifted(enc_local, 1), shifted(enc_local, -1)])
    per_dev = tok // WIN
    total = per_dev * lax.axis_size("space")
    reach = (neighbours - (block - 1) * per_dev) % total
    order = jnp.where(reach < per_dev, reach + per_dev, jnp.where(reach < 2 * per_dev, reach - per_dev, reach))
    return forecasts(
        order * WIN, grid3, enc3, dec_local, noise, w_in, w_gamma, w_beta, w_qkv, w_o, readout
    )


def body(
    grid_in, target, noise, neighbours, enc_index, dec_index,
    w_in, w_gamma, w_beta, w_qkv, w_o, readout_matrix,
):
    grid_dev = dec_index.shape[0]
    members_dev = noise.shape[1]
    predicted_quantities = grid_in[0]
    predicted_states, features = front(
        grid_in[0], noise[0], neighbours, enc_index, dec_index,
        w_in, w_gamma, w_beta, w_qkv, w_o, readout_matrix,
    )
    members_all = members_dev * lax.axis_size("member")
    ensemble_wide_entries = lax.all_gather(predicted_states, "member", axis=0, tiled=True)
    complete_quantities = ensemble_wide_entries.astype(F32)
    resident_quantities = predicted_states.astype(F32)
    truth = target[0].astype(F32)
    truth_sq = jnp.sum((resident_quantities - truth) ** 2, axis=(1, 2))
    pair_sq = jnp.sum((resident_quantities[:, None] - complete_quantities[None]) ** 2, axis=(2, 3))
    truth_sq, pair_sq = lax.psum((truth_sq, pair_sq), "space")
    to_truth = jnp.sqrt(truth_sq + EPSILON)
    pair_dist = jnp.sqrt(pair_sq + EPSILON)
    own_ids = lax.axis_index("member") * members_dev + jnp.arange(members_dev, dtype=jnp.int32)
    pair_mask = (jnp.arange(members_all, dtype=jnp.int32)[None, :] != own_ids[:, None]).astype(F32)
    score_part = jnp.sum(to_truth) / members_all - jnp.sum(pair_dist * pair_mask) / (
        2.0 * members_all * members_all
    )
    score_sum = lax.psum(score_part, ("dp", "member"))
    grid_total = grid_dev * lax.axis_size("space")
    objective_mean = score_sum / (
        lax.axis_size("dp") * jnp.sqrt(jnp.float32(predicted_quantities.shape[0] * grid_total))
    )
    truth_pull = 1.0 / (members_all * to_truth)
    pair_pull = pair_mask / (members_all * members_all * pair_dist)
    slope_bf = (
        truth_pull[:, None, None] * (resident_quantities - truth)
        - jnp.sum(pair_pull, axis=1)[:, None, None] * resident_quantities
        + jnp.einsum("mn,nvg->mvg", pair_pull, complete_quantities, precision=lax.Precision.HIGHEST)
    ).astype(BF16)
    partial_value = jnp.einsum("mvg,mgd->vd", slope_bf, features, preferred_element_type=F32)
    grad_share = lax.psum_scatter(
        partial_value.astype(BF16), "space", scatter_dimension=1, tiled=True
    ).astype(F32)
    grad_share = lax.psum(grad_share, ("dp", "member"))
    square = lax.psum(jnp.sum(grad_share * grad_share), "space")
    grad_piece = grad_share / jnp.sqrt(square / partial_value.size + EPSILON)
    unit_descent_slope = lax.all_gather(grad_piece, "space", axis=1, tiled=True)
    return (predicted_states[None], objective_mean, unit_descent_slope)


def solution(mesh):
    in_specs = (
        P("dp", None, "space"),
        P("dp", None, "space"),
        P("dp", "member", None),
        P("space", None),
        P("space", None),
        P("space", None),
        P(),
        P(),
        P(),
        P(),
        P(),
        P(),
    )
    out_specs = (P("dp", "member", None, "space"), P(), P())
    return jax.shard_map(body, mesh=mesh, in_specs=in_specs, out_specs=out_specs, check_vma=False)
```

```python
import functools

import jax
import jax.numpy as jnp
from jax import lax
from jax.experimental import pallas as pl
from jax.experimental.pallas import tpu as pltpu
from jax.sharding import PartitionSpec as P

HEADS = 12
HD = 64
WIN = 64
EPSILON = 1e-06
F32 = jnp.float32
BF16 = jnp.bfloat16
NT = (((1,), (1,)), ((), ()))
VMEM_LIMIT = 60000 * 1024


def parts(values):
    hi = values.astype(BF16)
    rest = values - hi.astype(F32)
    mid = rest.astype(BF16)
    lo = (rest - mid.astype(F32)).astype(BF16)
    return hi, mid, lo


def counts_of(index, targets):
    positions = lax.broadcasted_iota(jnp.int32, (index.shape[0], targets), 1)
    counts = jnp.zeros((index.shape[0], targets), F32)
    for column in range(index.shape[1]):
        counts = counts + jnp.where(index[:, column : column + 1] == positions, 1.0, 0.0)
    return counts.astype(BF16)


def member_kernel(
    reach_ref, grid_ref, enc_ref, dec_ref, noise_ref, w_in_ref, w_gamma_ref, w_beta_ref,
    w_qkv_ref, w_o_ref, readout_ref,
    pred_ref, feat_ref,
    states_ref, normed_ref, gain_ref, shift_ref, dec_counts_ref, bias_ref, q_ref, kv_ref, att_ref,
):
    m = pl.program_id(0)
    tok = enc_ref.shape[1]
    grid_dev = grid_ref.shape[2]
    d_model = w_o_ref.shape[0]
    k_enc = enc_ref.shape[2]
    k_dec = dec_ref.shape[1]
    windows = tok // WIN

    @pl.when(m == 0)
    def _():
        for block in range(3):
            counts = counts_of(enc_ref[block], grid_dev)
            pooled = lax.dot_general(counts, grid_ref[block], NT, preferred_element_type=F32)
            states = jnp.zeros((tok, d_model), F32)
            for part in parts(pooled):
                states = states + jnp.dot(part, w_in_ref[...], preferred_element_type=F32)
            states = states * (1.0 / k_enc)
            if block == 0:
                states_ref[...] = states
            centre = states - jnp.mean(states, axis=-1, keepdims=True)
            spread = jnp.mean(centre * centre, axis=-1, keepdims=True)
            normed_ref[block * tok : (block + 1) * tok, :] = centre / jnp.sqrt(spread + EPSILON)
        noise = noise_ref[...]
        gain_ref[...] = 1.0 + jnp.dot(
            noise, w_gamma_ref[...], precision=lax.Precision.HIGHEST, preferred_element_type=F32
        )
        shift_ref[...] = jnp.dot(
            noise, w_beta_ref[...], precision=lax.Precision.HIGHEST, preferred_element_type=F32
        )
        dec_counts_ref[...] = counts_of(dec_ref[...], tok)
        lane = lax.broadcasted_iota(jnp.int32, (WIN, 3 * tok), 1)
        for window in range(windows):
            lo = window * WIN
            open_keys = (lane >= lo) & (lane < lo + WIN)
            for slot in range(reach_ref.shape[1]):
                start = reach_ref[window, slot]
                open_keys = open_keys | ((lane >= start) & (lane < start + WIN))
            row = jnp.where(open_keys, 0.0, -jnp.inf).astype(F32)
            bias_ref[lo : lo + WIN, :] = row
            bias_ref[tok + lo : tok + lo + WIN, :] = row

    inputs = (normed_ref[...] * gain_ref[pl.ds(m, 1), :] + shift_ref[pl.ds(m, 1), :]).astype(BF16)
    q_ref[...] = jnp.dot(
        inputs[:tok], w_qkv_ref[:, :d_model], preferred_element_type=F32
    ).astype(BF16)
    kv_ref[...] = jnp.dot(
        inputs, w_qkv_ref[:, d_model:], preferred_element_type=F32
    ).astype(BF16)
    pair_lane = lax.broadcasted_iota(jnp.int32, (tok, 2 * HD), 1)
    first = jnp.where(pair_lane < HD, HD ** (-0.5), 0.0).astype(BF16)
    second = jnp.where(pair_lane < HD, 0.0, HD ** (-0.5)).astype(BF16)
    for pair in range(d_model // (2 * HD)):
        cols = slice(pair * 2 * HD, (pair + 1) * 2 * HD)
        q = q_ref[:, cols]
        both = jnp.concatenate([q * first, q * second], axis=0)
        scores = lax.dot_general(both, kv_ref[:, cols], NT, preferred_element_type=F32)
        scores = scores + bias_ref[...]
        e = jnp.exp(scores - jnp.max(scores, axis=-1, keepdims=True))
        weights = (e * (1.0 / jnp.sum(e, axis=-1, keepdims=True))).astype(BF16)
        v = kv_ref[:, d_model + pair * 2 * HD : d_model + (pair + 1) * 2 * HD]
        out = jnp.dot(weights, v, preferred_element_type=F32)
        att_ref[:, cols] = jnp.where(pair_lane < HD, out[:tok], out[tok:]).astype(BF16)
    updated = states_ref[...] + jnp.dot(att_ref[...], w_o_ref[...], preferred_element_type=F32)
    dec_counts = dec_counts_ref[...]
    features = (
        jnp.dot(
            jnp.concatenate([dec_counts] * 3, axis=1),
            jnp.concatenate(parts(updated), axis=0),
            preferred_element_type=F32,
        )
        * (1.0 / k_dec)
    ).astype(BF16)
    feat_ref[0] = features
    pred_ref[0] = (
        grid_ref[0].astype(F32)
        + lax.dot_general(readout_ref[...], features, NT, preferred_element_type=F32)
    ).astype(BF16)


def forecasts(reach, grid3, enc3, dec_local, noise, w_in, w_gamma, w_beta, w_qkv, w_o, readout):
    members = noise.shape[0]
    tok = enc3.shape[1]
    v_count, grid_dev = grid3.shape[1:]
    d_model = w_o.shape[0]
    whole = pl.BlockSpec(memory_space=pltpu.VMEM)
    return pl.pallas_call(
        member_kernel,
        grid=(members,),
        out_shape=(
            jax.ShapeDtypeStruct((members, v_count, grid_dev), BF16),
            jax.ShapeDtypeStruct((members, grid_dev, d_model), BF16),
        ),
        in_specs=[pl.BlockSpec(memory_space=pltpu.SMEM)] + [whole] * 10,
        out_specs=(
            pl.BlockSpec((1, v_count, grid_dev), lambda m: (m, 0, 0)),
            pl.BlockSpec((1, grid_dev, d_model), lambda m: (m, 0, 0)),
        ),
        scratch_shapes=[
            pltpu.VMEM((tok, d_model), F32),
            pltpu.VMEM((3 * tok, d_model), F32),
            pltpu.VMEM((members, d_model), F32),
            pltpu.VMEM((members, d_model), F32),
            pltpu.VMEM((grid_dev, tok), BF16),
            pltpu.VMEM((2 * tok, 3 * tok), F32),
            pltpu.VMEM((tok, d_model), BF16),
            pltpu.VMEM((3 * tok, 2 * d_model), BF16),
            pltpu.VMEM((tok, d_model), BF16),
        ],
        compiler_params=pltpu.CompilerParams(vmem_limit_bytes=VMEM_LIMIT),
        name="forecasts",
    )(reach, grid3, enc3, dec_local, noise, w_in, w_gamma, w_beta, w_qkv, w_o, readout)


def shifted(values, step):
    count = lax.axis_size("space")
    return lax.ppermute(values, "space", [(i, (i + step) % count) for i in range(count)])


def front(grid_in, noise, neighbours, enc_index, dec_index, w_in, w_gamma, w_beta, w_qkv, w_o, readout):
    tok = enc_index.shape[0]
    grid_dev = dec_index.shape[0]
    block = lax.axis_index("space")
    enc_local = enc_index - block * grid_dev
    dec_local = dec_index - block * tok
    grid3 = jnp.stack([grid_in, shifted(grid_in, 1), shifted(grid_in, -1)])
    enc3 = jnp.stack([enc_local, shifted(enc_local, 1), shifted(enc_local, -1)])
    per_dev = tok // WIN
    total = per_dev * lax.axis_size("space")
    reach = (neighbours - (block - 1) * per_dev) % total
    order = jnp.where(reach < per_dev, reach + per_dev, jnp.where(reach < 2 * per_dev, reach - per_dev, reach))
    return forecasts(
        order * WIN, grid3, enc3, dec_local, noise, w_in, w_gamma, w_beta, w_qkv, w_o, readout
    )


def own_device_scopes():
    return lax.axis_index("dp"), lax.axis_index("member"), lax.axis_index("space")


def tail_kernel(
    sizes, pred_ref, target_ref, feat_ref, score_ref, slope_out_ref,
    others_ref, dist_ref, grad_ref, share_out, share_in, mid_out, mid_in, full_ref,
    score_m, score_d,
    pred_s, pred_r, dist_s, dist_r, share_s, share_r, mid_s, mid_r, full_s, full_r,
    sm_s, sm_r, sd_s, sd_r,
):
    n_dp, n_member, n_space = sizes
    plane = n_member * n_space
    my_dp, my_member, my_space = own_device_scopes()
    me = my_member * n_space + my_space
    mine = pred_ref.shape[0]
    everyone = mine * n_member
    v_count, grid_dev = target_ref.shape
    rows = share_out.shape[1]
    pair_rows = mine * everyone

    def plane_peer(step):
        peer = lax.rem(me + step, plane)
        return peer, {"member": peer // n_space, "space": lax.rem(peer, n_space)}

    def send(src, dst, s_sem, r_sem, target):
        copy = pltpu.make_async_remote_copy(
            src_ref=src, dst_ref=dst, send_sem=s_sem, recv_sem=r_sem,
            device_id=target, device_id_type=pl.DeviceIdType.MESH,
        )
        copy.start()
        return copy

    barrier = pltpu.get_barrier_semaphore()
    for step in range(1, plane):
        pl.semaphore_signal(
            barrier, inc=1, device_id=plane_peer(step)[1], device_id_type=pl.DeviceIdType.MESH
        )
    for step in range(1, n_dp):
        pl.semaphore_signal(
            barrier, inc=1, device_id={"dp": lax.rem(my_dp + step, n_dp)},
            device_id_type=pl.DeviceIdType.MESH,
        )
    pl.semaphore_wait(barrier, plane - 1 + n_dp - 1)

    pred_copies = []
    for step in range(1, n_member):
        target = {"member": lax.rem(my_member + step, n_member)}
        pred_copies.append(
            send(pred_ref, others_ref.at[step - 1], pred_s.at[step - 1], pred_r.at[step - 1], target)
        )

    def resident(n):
        if n < mine:
            return pred_ref[n].astype(F32)
        return others_ref[n // mine - 1, n % mine].astype(F32)

    def squares(left, right):
        gap = left - right
        line = jnp.sum(gap * gap, axis=0, keepdims=True)
        total = line[:, :128]
        for lane in range(128, grid_dev, 128):
            total = total + line[:, lane : lane + 128]
        return total

    dist_ref[my_space] = jnp.zeros(dist_ref.shape[1:], F32)
    truth = target_ref[...].astype(F32)
    for m in range(mine):
        x = resident(m)
        dist_ref[my_space, pair_rows + m : pair_rows + m + 1, :] = squares(x, truth)
        for n in range(m + 1, mine):
            line = squares(x, resident(n))
            for row in (m * everyone + n, n * everyone + m):
                dist_ref[my_space, row : row + 1, :] = line
    for copy in pred_copies:
        copy.wait()
    for m in range(mine):
        x = resident(m)
        for n in range(mine, everyone):
            row = m * everyone + n
            dist_ref[my_space, row : row + 1, :] = squares(x, resident(n))
    copies = []
    for step in range(1, n_space):
        target = {"space": lax.rem(my_space + step, n_space)}
        copies.append(
            send(dist_ref.at[my_space], dist_ref.at[my_space], dist_s.at[step - 1], dist_r.at[step - 1], target)
        )
    for copy in copies:
        copy.wait()
    total = dist_ref[0]
    for s in range(1, n_space):
        total = total + dist_ref[s]
    dist = jnp.sqrt(jnp.sum(total, axis=-1, keepdims=True) + EPSILON)
    pull = 1.0 / dist
    row_id = lax.broadcasted_iota(jnp.int32, dist.shape, 0)
    share = jnp.where(row_id < pair_rows, -1.0 / (2.0 * everyone * everyone), 1.0 / everyone)
    share = jnp.where(row_id >= pair_rows + mine, 0.0, share)
    for m in range(mine):
        share = jnp.where(row_id == m * everyone + m, 0.0, share)
    score = jnp.sum(dist * share, axis=0, keepdims=True)
    score_m[my_member] = jnp.broadcast_to(score, score_m.shape[1:])
    copies = []
    for step in range(1, n_member):
        target = {"member": lax.rem(my_member + step, n_member)}
        copies.append(
            send(score_m.at[my_member], score_m.at[my_member], sm_s.at[step - 1], sm_r.at[step - 1], target)
        )
    grad = jnp.zeros((v_count, feat_ref.shape[2]), F32)
    for m in range(mine):
        x = resident(m)
        truth_pull = pull[pair_rows + m : pair_rows + m + 1, :] * (1.0 / everyone)
        slope = truth_pull * (x - truth)
        own_pull = jnp.zeros((1, 1), F32)
        mixed = jnp.zeros_like(x)
        for n in range(everyone):
            if n != m:
                row = m * everyone + n
                b = pull[row : row + 1, :] * (1.0 / (everyone * everyone))
                own_pull = own_pull + b
                mixed = mixed + b * resident(n)
        slope = (slope - own_pull * x + mixed).astype(BF16)
        grad = grad + jnp.dot(slope, feat_ref[m], preferred_element_type=F32)
    grad_ref[v_count:, :] = jnp.zeros((grad_ref.shape[0] - v_count, grad_ref.shape[1]), F32)
    grad_ref[:v_count, :] = grad
    for owner in range(plane):
        share_out[owner] = grad_ref[owner * rows : (owner + 1) * rows, :].astype(BF16)
    share_copies = []
    for step in range(1, plane):
        peer, target = plane_peer(step)
        share_copies.append(
            send(share_out.at[peer], share_in.at[me], share_s.at[step - 1], share_r.at[step - 1], target)
        )
    share_in[me] = share_out[me]
    for copy in copies:
        copy.wait()
    total = score_m[0]
    for s in range(1, n_member):
        total = total + score_m[s]
    score_d[my_dp] = total
    copies = []
    for step in range(1, n_dp):
        target = {"dp": lax.rem(my_dp + step, n_dp)}
        copies.append(
            send(score_d.at[my_dp], score_d.at[my_dp], sd_s.at[step - 1], sd_r.at[step - 1], target)
        )
    for copy in share_copies:
        copy.wait()
    total = share_in[0].astype(F32)
    for s in range(1, plane):
        total = total + share_in[s].astype(F32)
    mid_in[my_dp] = total.astype(BF16)
    mid_copies = []
    for step in range(1, n_dp):
        target = {"dp": lax.rem(my_dp + step, n_dp)}
        mid_copies.append(
            send(mid_in.at[my_dp], mid_in.at[my_dp], mid_s.at[step - 1], mid_r.at[step - 1], target)
        )
    for copy in copies:
        copy.wait()
    total = score_d[0]
    for s in range(1, n_dp):
        total = total + score_d[s]
    grid_total = grid_dev * n_space
    score_ref[...] = total / (n_dp * jnp.sqrt(jnp.full(total.shape, float(v_count * grid_total), F32)))
    for copy in mid_copies:
        copy.wait()
    total = mid_in[0].astype(F32)
    for s in range(1, n_dp):
        total = total + mid_in[s].astype(F32)
    full_ref[me] = total
    copies = []
    for step in range(1, plane):
        copies.append(
            send(full_ref.at[me], full_ref.at[me], full_s.at[step - 1], full_r.at[step - 1], plane_peer(step)[1])
        )
    for copy in copies:
        copy.wait()
    square = jnp.zeros((1, full_ref.shape[2]), F32)
    for owner in range(plane):
        piece = full_ref[owner]
        square = square + jnp.sum(piece * piece, axis=0, keepdims=True)
    square = jnp.sum(square, axis=-1, keepdims=True)
    scale = 1.0 / jnp.sqrt(square / (v_count * full_ref.shape[2]) + EPSILON)
    for owner in range(plane):
        keep = min(rows, v_count - owner * rows)
        if keep > 0:
            slope_out_ref[owner * rows : owner * rows + keep, :] = full_ref[owner, :keep, :] * scale


def energy_tail(pred, target, features):
    sizes = tuple(lax.axis_size(name) for name in ("dp", "member", "space"))
    n_dp, n_member, n_space = sizes
    plane = n_member * n_space
    mine, v_count, grid_dev = pred.shape
    d_model = features.shape[2]
    rows = -(-v_count // plane)
    dist_rows = -(-(mine * mine * n_member + mine) // 8) * 8
    grad_rows = max(plane * rows, v_count + 1)
    whole = pl.BlockSpec(memory_space=pltpu.VMEM)

    def sems(count):
        return [pltpu.SemaphoreType.DMA((count,))] * 2

    return pl.pallas_call(
        functools.partial(tail_kernel, sizes),
        out_shape=(
            jax.ShapeDtypeStruct((8, 128), F32),
            jax.ShapeDtypeStruct((v_count, d_model), F32),
        ),
        in_specs=[whole] * 3,
        out_specs=(whole, whole),
        scratch_shapes=[
            pltpu.VMEM((n_member - 1, mine, v_count, grid_dev), BF16),
            pltpu.VMEM((n_space, dist_rows, 128), F32),
            pltpu.VMEM((grad_rows, d_model), F32),
            pltpu.VMEM((plane, rows, d_model), BF16),
            pltpu.VMEM((plane, rows, d_model), BF16),
            pltpu.VMEM((rows, d_model), BF16),
            pltpu.VMEM((n_dp, rows, d_model), BF16),
            pltpu.VMEM((plane, rows, d_model), F32),
            pltpu.VMEM((n_member, 8, 128), F32),
            pltpu.VMEM((n_dp, 8, 128), F32),
        ]
        + sems(n_member - 1) + sems(n_space - 1) + sems(plane - 1) + sems(n_dp - 1)
        + sems(plane - 1) + sems(n_member - 1) + sems(n_dp - 1),
        compiler_params=pltpu.CompilerParams(
            collective_id=0, has_side_effects=True, vmem_limit_bytes=VMEM_LIMIT
        ),
        name="energy_tail",
    )(pred, target, features)


def body(
    grid_in, target, noise, neighbours, enc_index, dec_index,
    w_in, w_gamma, w_beta, w_qkv, w_o, readout_matrix,
):
    predicted_states, features = front(
        grid_in[0], noise[0], neighbours, enc_index, dec_index,
        w_in, w_gamma, w_beta, w_qkv, w_o, readout_matrix,
    )
    score, unit_descent_slope = energy_tail(predicted_states, target[0], features)
    return (predicted_states[None], score[0, 0], unit_descent_slope)


def solution(mesh):
    in_specs = (
        P("dp", None, "space"),
        P("dp", None, "space"),
        P("dp", "member", None),
        P("space", None),
        P("space", None),
        P("space", None),
        P(),
        P(),
        P(),
        P(),
        P(),
        P(),
    )
    out_specs = (P("dp", "member", None, "space"), P(), P())
    return jax.shard_map(body, mesh=mesh, in_specs=in_specs, out_specs=out_specs, check_vma=False)
```

```python
import functools

import jax
import jax.numpy as jnp
from jax import lax
from jax.experimental import pallas as pl
from jax.experimental.pallas import tpu as pltpu
from jax.sharding import PartitionSpec as P

HEADS = 12
HD = 64
WIN = 64
EPSILON = 1e-06
F32 = jnp.float32
BF16 = jnp.bfloat16
NT = (((1,), (1,)), ((), ()))
VMEM_LIMIT = 60000 * 1024


def parts(values):
    hi = values.astype(BF16)
    rest = values - hi.astype(F32)
    mid = rest.astype(BF16)
    lo = (rest - mid.astype(F32)).astype(BF16)
    return hi, mid, lo


def counts_of(index, targets):
    positions = lax.broadcasted_iota(jnp.int32, (targets, index.shape[1]), 0)
    counts = jnp.zeros((targets, index.shape[1]), F32)
    for column in range(index.shape[0]):
        counts = counts + jnp.where(index[column : column + 1, :] == positions, 1.0, 0.0)
    return counts


def window_kernel(
    sizes,
    neighbours_ref, grid_ref, enc_ref, dec_ref, noise_ref,
    target_hbm, w_in_hbm, w_gamma_hbm, w_beta_hbm, w_qkv_hbm, w_o_hbm, readout_hbm,
    pred_ref, score_ref, slope_out_ref,
    target_ref, w_in_ref, w_gamma_ref, w_beta_ref, w_qkv_ref, w_o_ref, readout_ref, load_sem,
    side_grid, side_enc, side_s, side_r,
    states_ref, normed_ref, gain_ref, shift_ref, dec_counts_ref, bias_ref, q_ref, kv_ref, att_ref,
    feat_ref,
    others_ref, dist_ref, grad_ref, share_out, share_in, mid_in, full_ref,
    score_m, score_d,
    pred_s, pred_r, dist_s, dist_r, share_s, share_r, mid_s, mid_r, full_s, full_r,
    sm_s, sm_r, sd_s, sd_r,
):
    n_dp, n_member, n_space = sizes
    plane = n_member * n_space
    my_dp = lax.axis_index("dp")
    my_member = lax.axis_index("member")
    my_space = lax.axis_index("space")
    me = my_member * n_space + my_space
    mine = pred_ref.shape[0]
    everyone = mine * n_member
    v_count, grid_dev = target_ref.shape
    rows = share_out.shape[1]
    pair_rows = mine * everyone
    k_enc, tok = enc_ref.shape
    k_dec = dec_ref.shape[0]
    d_model = w_o_ref.shape[0]
    windows = tok // WIN

    def plane_peer(step):
        peer = lax.rem(me + step, plane)
        return peer, {"member": peer // n_space, "space": lax.rem(peer, n_space)}

    def remote(src, dst, s_sem, r_sem, target):
        return pltpu.make_async_remote_copy(
            src_ref=src, dst_ref=dst, send_sem=s_sem, recv_sem=r_sem,
            device_id=target, device_id_type=pl.DeviceIdType.MESH,
        )

    def send(*args):
        copy = remote(*args)
        copy.start()
        return copy

    barrier = pltpu.get_barrier_semaphore()
    for step in range(1, plane):
        pl.semaphore_signal(
            barrier, inc=1, device_id=plane_peer(step)[1], device_id_type=pl.DeviceIdType.MESH
        )
    for step in range(1, n_dp):
        pl.semaphore_signal(
            barrier, inc=1, device_id={"dp": lax.rem(my_dp + step, n_dp)},
            device_id_type=pl.DeviceIdType.MESH,
        )
    loads = []
    for src, dst in (
        (w_in_hbm, w_in_ref), (w_gamma_hbm, w_gamma_ref), (w_beta_hbm, w_beta_ref),
        (w_qkv_hbm, w_qkv_ref), (w_o_hbm, w_o_ref), (readout_hbm, readout_ref),
        (target_hbm, target_ref),
    ):
        loads.append(pltpu.make_async_copy(src, dst, load_sem.at[len(loads)]))
        loads[-1].start()
    pl.semaphore_wait(barrier, plane - 1 + n_dp - 1)

    side_copies = []
    for slot, step in ((0, 1), (1, n_space - 1)):
        target = {"space": lax.rem(my_space + step, n_space)}
        side_copies.append(
            send(grid_ref, side_grid.at[slot], side_s.at[2 * slot], side_r.at[2 * slot], target)
        )
        side_copies.append(
            send(enc_ref, side_enc.at[slot], side_s.at[2 * slot + 1], side_r.at[2 * slot + 1], target)
        )

    def encode(block, grid_values, index, base):
        counts = counts_of(index - base, grid_dev).astype(BF16)
        pooled = jnp.dot(grid_values, counts, preferred_element_type=F32)
        states = jnp.zeros((tok, d_model), F32)
        for part in parts(pooled):
            states = states + lax.dot_general(
                part, w_in_ref[...], (((0,), (0,)), ((), ())), preferred_element_type=F32
            )
        states = states * (1.0 / k_enc)
        if block == 0:
            states_ref[...] = states
        centre = states - jnp.mean(states, axis=-1, keepdims=True)
        spread = jnp.mean(centre * centre, axis=-1, keepdims=True)
        normed_ref[block * tok : (block + 1) * tok, :] = centre / jnp.sqrt(spread + EPSILON)

    dec_counts_ref[...] = jnp.transpose(counts_of(dec_ref[...] - my_space * tok, tok)).astype(BF16)
    lane = lax.broadcasted_iota(jnp.int32, (WIN, 3 * tok), 1)
    total_windows = windows * n_space
    for window in range(windows):
        lo = window * WIN
        open_keys = (lane >= lo) & (lane < lo + WIN)
        for slot in range(neighbours_ref.shape[1]):
            reach = lax.rem(
                neighbours_ref[window, slot] - (my_space - 1) * windows + total_windows, total_windows
            )
            place = jnp.where(
                reach < windows, reach + windows, jnp.where(reach < 2 * windows, reach - windows, reach)
            )
            start = place * WIN
            open_keys = open_keys | ((lane >= start) & (lane < start + WIN))
        row = jnp.where(open_keys, 0.0, -jnp.inf).astype(F32)
        bias_ref[lo : lo + WIN, :] = row
        bias_ref[tok + lo : tok + lo + WIN, :] = row
    for load in loads[:3]:
        load.wait()
    noise = noise_ref[...]
    gain_ref[...] = 1.0 + jnp.dot(
        noise, w_gamma_ref[...], precision=lax.Precision.HIGHEST, preferred_element_type=F32
    )
    shift_ref[...] = jnp.dot(
        noise, w_beta_ref[...], precision=lax.Precision.HIGHEST, preferred_element_type=F32
    )
    encode(0, grid_ref[...], enc_ref[...], my_space * grid_dev)
    for copy in side_copies:
        copy.wait()
    encode(1, side_grid[0], side_enc[0], lax.rem(my_space + n_space - 1, n_space) * grid_dev)
    encode(2, side_grid[1], side_enc[1], lax.rem(my_space + 1, n_space) * grid_dev)
    for load in loads[3:]:
        load.wait()

    def pred_copy(m, step):
        slot = m * (n_member - 1) + step - 1
        target = {"member": lax.rem(my_member + step, n_member)}
        return remote(
            pred_ref.at[m], others_ref.at[step - 1, m], pred_s.at[slot], pred_r.at[slot], target
        )

    pair_lane = lax.broadcasted_iota(jnp.int32, (tok, 2 * HD), 1)
    first = jnp.where(pair_lane < HD, HD ** (-0.5), 0.0).astype(BF16)
    second = jnp.where(pair_lane < HD, 0.0, HD ** (-0.5)).astype(BF16)

    def one_member(m, carry):
        inputs = (
            normed_ref[...] * gain_ref[pl.ds(m, 1), :] + shift_ref[pl.ds(m, 1), :]
        ).astype(BF16)
        q_ref[...] = jnp.dot(
            inputs[:tok], w_qkv_ref[:, :d_model], preferred_element_type=F32
        ).astype(BF16)
        kv_ref[...] = jnp.dot(
            inputs, w_qkv_ref[:, d_model:], preferred_element_type=F32
        ).astype(BF16)
        for pair in range(d_model // (2 * HD)):
            cols = slice(pair * 2 * HD, (pair + 1) * 2 * HD)
            q = q_ref[:, cols]
            both = jnp.concatenate([q * first, q * second], axis=0)
            scores = lax.dot_general(both, kv_ref[:, cols], NT, preferred_element_type=F32)
            scores = scores + bias_ref[...]
            e = jnp.exp(scores - jnp.max(scores, axis=-1, keepdims=True))
            weights = (e * (1.0 / jnp.sum(e, axis=-1, keepdims=True))).astype(BF16)
            v = kv_ref[:, d_model + pair * 2 * HD : d_model + (pair + 1) * 2 * HD]
            out = jnp.dot(weights, v, preferred_element_type=F32)
            att_ref[:, cols] = jnp.where(pair_lane < HD, out[:tok], out[tok:]).astype(BF16)
        updated = states_ref[...] + jnp.dot(att_ref[...], w_o_ref[...], preferred_element_type=F32)
        dec_counts = dec_counts_ref[...]
        features = (
            jnp.dot(
                jnp.concatenate([dec_counts] * 3, axis=1),
                jnp.concatenate(parts(updated), axis=0),
                preferred_element_type=F32,
            )
            * (1.0 / k_dec)
        ).astype(BF16)
        feat_ref[m] = features
        pred_ref[m] = (
            grid_ref[...].astype(F32)
            + lax.dot_general(readout_ref[...], features, NT, preferred_element_type=F32)
        ).astype(BF16)
        for step in range(1, n_member):
            pred_copy(m, step).start()
        return carry

    lax.fori_loop(0, mine, one_member, 0)

    def resident(n):
        if n < mine:
            return pred_ref[n].astype(F32)
        return others_ref[n // mine - 1, n % mine].astype(F32)

    def squares(left, right):
        gap = left - right
        line = jnp.sum(gap * gap, axis=0, keepdims=True)
        total = line[:, :128]
        for lane in range(128, grid_dev, 128):
            total = total + line[:, lane : lane + 128]
        return total

    dist_ref[my_space] = jnp.zeros(dist_ref.shape[1:], F32)
    truth = target_ref[...].astype(F32)
    for m in range(mine):
        x = resident(m)
        dist_ref[my_space, pair_rows + m : pair_rows + m + 1, :] = squares(x, truth)
        for n in range(m + 1, mine):
            line = squares(x, resident(n))
            for row in (m * everyone + n, n * everyone + m):
                dist_ref[my_space, row : row + 1, :] = line
    for m in range(mine):
        for step in range(1, n_member):
            pred_copy(m, step).wait()
    for m in range(mine):
        x = resident(m)
        for n in range(mine, everyone):
            row = m * everyone + n
            dist_ref[my_space, row : row + 1, :] = squares(x, resident(n))
    copies = []
    for step in range(1, n_space):
        target = {"space": lax.rem(my_space + step, n_space)}
        copies.append(
            send(dist_ref.at[my_space], dist_ref.at[my_space], dist_s.at[step - 1], dist_r.at[step - 1], target)
        )
    for copy in copies:
        copy.wait()
    total = dist_ref[0]
    for s in range(1, n_space):
        total = total + dist_ref[s]
    dist = jnp.sqrt(jnp.sum(total, axis=-1, keepdims=True) + EPSILON)
    pull = 1.0 / dist
    row_id = lax.broadcasted_iota(jnp.int32, dist.shape, 0)
    share = jnp.where(row_id < pair_rows, -1.0 / (2.0 * everyone * everyone), 1.0 / everyone)
    share = jnp.where(row_id >= pair_rows + mine, 0.0, share)
    for m in range(mine):
        share = jnp.where(row_id == m * everyone + m, 0.0, share)
    score = jnp.sum(dist * share, axis=0, keepdims=True)
    score_m[my_member] = jnp.broadcast_to(score, score_m.shape[1:])
    copies = []
    for step in range(1, n_member):
        target = {"member": lax.rem(my_member + step, n_member)}
        copies.append(
            send(score_m.at[my_member], score_m.at[my_member], sm_s.at[step - 1], sm_r.at[step - 1], target)
        )
    grad = jnp.zeros((v_count, feat_ref.shape[2]), F32)
    for m in range(mine):
        x = resident(m)
        truth_pull = pull[pair_rows + m : pair_rows + m + 1, :] * (1.0 / everyone)
        slope = truth_pull * (x - truth)
        own_pull = jnp.zeros((1, 1), F32)
        mixed = jnp.zeros_like(x)
        for n in range(everyone):
            if n != m:
                row = m * everyone + n
                b = pull[row : row + 1, :] * (1.0 / (everyone * everyone))
                own_pull = own_pull + b
                mixed = mixed + b * resident(n)
        slope = (slope - own_pull * x + mixed).astype(BF16)
        grad = grad + jnp.dot(slope, feat_ref[m], preferred_element_type=F32)
    grad_ref[v_count:, :] = jnp.zeros((grad_ref.shape[0] - v_count, grad_ref.shape[1]), F32)
    grad_ref[:v_count, :] = grad
    for owner in range(plane):
        share_out[owner] = grad_ref[owner * rows : (owner + 1) * rows, :].astype(BF16)
    share_copies = []
    for step in range(1, plane):
        peer, target = plane_peer(step)
        share_copies.append(
            send(share_out.at[peer], share_in.at[me], share_s.at[step - 1], share_r.at[step - 1], target)
        )
    share_in[me] = share_out[me]
    for copy in copies:
        copy.wait()
    total = score_m[0]
    for s in range(1, n_member):
        total = total + score_m[s]
    score_d[my_dp] = total
    copies = []
    for step in range(1, n_dp):
        target = {"dp": lax.rem(my_dp + step, n_dp)}
        copies.append(
            send(score_d.at[my_dp], score_d.at[my_dp], sd_s.at[step - 1], sd_r.at[step - 1], target)
        )
    for copy in share_copies:
        copy.wait()
    total = share_in[0].astype(F32)
    for s in range(1, plane):
        total = total + share_in[s].astype(F32)
    mid_in[my_dp] = total.astype(BF16)
    mid_copies = []
    for step in range(1, n_dp):
        target = {"dp": lax.rem(my_dp + step, n_dp)}
        mid_copies.append(
            send(mid_in.at[my_dp], mid_in.at[my_dp], mid_s.at[step - 1], mid_r.at[step - 1], target)
        )
    for copy in copies:
        copy.wait()
    total = score_d[0]
    for s in range(1, n_dp):
        total = total + score_d[s]
    grid_total = grid_dev * n_space
    total = total / (n_dp * jnp.sqrt(jnp.full(total.shape, float(v_count * grid_total), F32)))
    score_ref[0, 0] = jnp.max(total)
    for copy in mid_copies:
        copy.wait()
    total = mid_in[0].astype(F32)
    for s in range(1, n_dp):
        total = total + mid_in[s].astype(F32)
    full_ref[me] = total
    copies = []
    for step in range(1, plane):
        copies.append(
            send(full_ref.at[me], full_ref.at[me], full_s.at[step - 1], full_r.at[step - 1], plane_peer(step)[1])
        )
    for copy in copies:
        copy.wait()
    square = jnp.zeros((1, full_ref.shape[2]), F32)
    for owner in range(plane):
        piece = full_ref[owner]
        square = square + jnp.sum(piece * piece, axis=0, keepdims=True)
    square = jnp.sum(square, axis=-1, keepdims=True)
    scale = 1.0 / jnp.sqrt(square / (v_count * full_ref.shape[2]) + EPSILON)
    for owner in range(plane):
        keep = min(rows, v_count - owner * rows)
        if keep > 0:
            slope_out_ref[owner * rows : owner * rows + keep, :] = full_ref[owner, :keep, :] * scale


def solution(mesh):
    sizes = tuple(mesh.shape[name] for name in ("dp", "member", "space"))
    n_dp, n_member, n_space = sizes
    plane = n_member * n_space

    def body(
        grid_in, target, noise, neighbours, enc_index, dec_index,
        w_in, w_gamma, w_beta, w_qkv, w_o, readout_matrix,
    ):
        v_count, grid_dev = target.shape[1:]
        mine = noise.shape[1]
        d_model = w_o.shape[0]
        tok = enc_index.shape[0]
        rows = -(-v_count // plane)
        dist_rows = -(-(mine * mine * n_member + mine) // 8) * 8
        grad_rows = max(plane * rows, v_count + 1)
        whole = pl.BlockSpec(memory_space=pltpu.VMEM)
        smem = pl.BlockSpec(memory_space=pltpu.SMEM)
        away = pl.BlockSpec(memory_space=pl.ANY)

        def sems(count):
            return [pltpu.SemaphoreType.DMA((count,))] * 2

        loaded = (target[0], w_in, w_gamma, w_beta, w_qkv, w_o, readout_matrix)
        pred, score, slope = pl.pallas_call(
            functools.partial(window_kernel, sizes),
            out_shape=(
                jax.ShapeDtypeStruct((mine, v_count, grid_dev), BF16),
                jax.ShapeDtypeStruct((1, 1), F32),
                jax.ShapeDtypeStruct((v_count, d_model), F32),
            ),
            in_specs=[smem] + [whole] * 4 + [away] * len(loaded),
            out_specs=(whole, smem, whole),
            scratch_shapes=[pltpu.VMEM(x.shape, x.dtype) for x in loaded]
            + [
                pltpu.SemaphoreType.DMA((len(loaded),)),
                pltpu.VMEM((2, v_count, grid_dev), BF16),
                pltpu.VMEM((2,) + enc_index.shape[::-1], jnp.int32),
            ]
            + sems(4)
            + [
                pltpu.VMEM((tok, d_model), F32),
                pltpu.VMEM((3 * tok, d_model), F32),
                pltpu.VMEM((mine, d_model), F32),
                pltpu.VMEM((mine, d_model), F32),
                pltpu.VMEM((grid_dev, tok), BF16),
                pltpu.VMEM((2 * tok, 3 * tok), F32),
                pltpu.VMEM((tok, d_model), BF16),
                pltpu.VMEM((3 * tok, 2 * d_model), BF16),
                pltpu.VMEM((tok, d_model), BF16),
                pltpu.VMEM((mine, grid_dev, d_model), BF16),
                pltpu.VMEM((n_member - 1, mine, v_count, grid_dev), BF16),
                pltpu.VMEM((n_space, dist_rows, 128), F32),
                pltpu.VMEM((grad_rows, d_model), F32),
                pltpu.VMEM((plane, rows, d_model), BF16),
                pltpu.VMEM((plane, rows, d_model), BF16),
                pltpu.VMEM((n_dp, rows, d_model), BF16),
                pltpu.VMEM((plane, rows, d_model), F32),
                pltpu.VMEM((n_member, 8, 128), F32),
                pltpu.VMEM((n_dp, 8, 128), F32),
            ]
            + sems((n_member - 1) * mine) + sems(n_space - 1) + sems(plane - 1) + sems(n_dp - 1)
            + sems(plane - 1) + sems(n_member - 1) + sems(n_dp - 1),
            compiler_params=pltpu.CompilerParams(
                collective_id=0, has_side_effects=True, vmem_limit_bytes=VMEM_LIMIT
            ),
            name="training_window",
        )(
            neighbours, grid_in[0], enc_index.T, dec_index.T, noise[0], *loaded
        )
        return (pred[None], score[0, 0], slope)

    in_specs = (
        P("dp", None, "space"),
        P("dp", None, "space"),
        P("dp", "member", None),
        P("space", None),
        P("space", None),
        P("space", None),
        P(),
        P(),
        P(),
        P(),
        P(),
        P(),
    )
    out_specs = (P("dp", "member", None, "space"), P(), P())
    return jax.shard_map(body, mesh=mesh, in_specs=in_specs, out_specs=out_specs, check_vma=False)
```

```python
import functools

import jax
import jax.numpy as jnp
from jax import lax
from jax.experimental import pallas as pl
from jax.experimental.pallas import tpu as pltpu
from jax.sharding import PartitionSpec as P

HEADS = 12
HD = 64
WIN = 64
CHUNK = 256
EPSILON = 1e-06
F32 = jnp.float32
BF16 = jnp.bfloat16
NT = (((1,), (1,)), ((), ()))
VMEM_LIMIT = 60000 * 1024


def parts(values):
    hi = values.astype(BF16)
    rest = values - hi.astype(F32)
    mid = rest.astype(BF16)
    lo = (rest - mid.astype(F32)).astype(BF16)
    return hi, mid, lo


def counts_of(index, targets):
    positions = lax.broadcasted_iota(jnp.int32, (targets, index.shape[1]), 0)
    counts = jnp.zeros((targets, index.shape[1]), F32)
    for column in range(index.shape[0]):
        counts = counts + jnp.where(index[column : column + 1, :] == positions, 1.0, 0.0)
    return counts


def window_kernel(
    sizes,
    neighbours_ref, grid_ref, enc_ref, dec_ref, noise_ref,
    target_hbm, w_in_hbm, w_gamma_hbm, w_beta_hbm, w_qkv_hbm, w_o_hbm, readout_hbm,
    pred_ref, score_ref, slope_out_ref,
    target_ref, w_in_ref, w_gamma_ref, w_beta_ref, w_qkv_ref, w_o_ref, readout_ref, load_sem,
    side_grid, side_enc, side_s, side_r,
    states_ref, normed_ref, gain_ref, shift_ref, dec_counts_ref, bias_ref, inputs_ref, q_ref, kv_ref, att_ref,
    feat_ref,
    others_ref, dist_ref, grad_ref, share_out, share_in, mid_in, full_ref,
    score_m, score_d,
    pred_s, pred_r, dist_s, dist_r, share_s, share_r, mid_s, mid_r, full_s, full_r,
    sm_s, sm_r, sd_s, sd_r,
):
    n_dp, n_member, n_space = sizes
    plane = n_member * n_space
    my_dp = lax.axis_index("dp")
    my_member = lax.axis_index("member")
    my_space = lax.axis_index("space")
    me = my_member * n_space + my_space
    mine = pred_ref.shape[0]
    everyone = mine * n_member
    v_count, grid_dev = target_ref.shape
    rows = share_out.shape[1]
    pair_rows = mine * everyone
    k_enc, tok = enc_ref.shape
    k_dec = dec_ref.shape[0]
    d_model = w_o_ref.shape[0]
    windows = tok // WIN

    def plane_peer(step):
        peer = lax.rem(me + step, plane)
        return peer, {"member": peer // n_space, "space": lax.rem(peer, n_space)}

    def remote(src, dst, s_sem, r_sem, target):
        return pltpu.make_async_remote_copy(
            src_ref=src, dst_ref=dst, send_sem=s_sem, recv_sem=r_sem,
            device_id=target, device_id_type=pl.DeviceIdType.MESH,
        )

    def send(*args):
        copy = remote(*args)
        copy.start()
        return copy

    barrier = pltpu.get_barrier_semaphore()
    for step in range(1, plane):
        pl.semaphore_signal(
            barrier, inc=1, device_id=plane_peer(step)[1], device_id_type=pl.DeviceIdType.MESH
        )
    for step in range(1, n_dp):
        pl.semaphore_signal(
            barrier, inc=1, device_id={"dp": lax.rem(my_dp + step, n_dp)},
            device_id_type=pl.DeviceIdType.MESH,
        )
    loads = []
    for src, dst in (
        (w_in_hbm, w_in_ref), (w_gamma_hbm, w_gamma_ref), (w_beta_hbm, w_beta_ref),
        (w_qkv_hbm, w_qkv_ref), (w_o_hbm, w_o_ref), (readout_hbm, readout_ref),
        (target_hbm, target_ref),
    ):
        loads.append(pltpu.make_async_copy(src, dst, load_sem.at[len(loads)]))
        loads[-1].start()
    def encode(block, grid_values, index, base):
        counts = counts_of(index - base, grid_dev).astype(BF16)
        pooled = jnp.dot(grid_values, counts, preferred_element_type=F32)
        states = jnp.zeros((tok, d_model), F32)
        for part in parts(pooled):
            states = states + lax.dot_general(
                part, w_in_ref[...], (((0,), (0,)), ((), ())), preferred_element_type=F32
            )
        states = states * (1.0 / k_enc)
        if block == 0:
            states_ref[...] = states
        centre = states - jnp.mean(states, axis=-1, keepdims=True)
        spread = jnp.mean(centre * centre, axis=-1, keepdims=True)
        normed_ref[block * tok : (block + 1) * tok, :] = centre / jnp.sqrt(spread + EPSILON)

    dec_counts_ref[...] = jnp.transpose(counts_of(dec_ref[...] - my_space * tok, tok)).astype(BF16)
    lane = lax.broadcasted_iota(jnp.int32, (WIN, 3 * tok), 1)
    total_windows = windows * n_space
    for window in range(windows):
        lo = window * WIN
        open_keys = (lane >= lo) & (lane < lo + WIN)
        for slot in range(neighbours_ref.shape[1]):
            reach = lax.rem(
                neighbours_ref[window, slot] - (my_space - 1) * windows + total_windows, total_windows
            )
            place = jnp.where(
                reach < windows, reach + windows, jnp.where(reach < 2 * windows, reach - windows, reach)
            )
            start = place * WIN
            open_keys = open_keys | ((lane >= start) & (lane < start + WIN))
        row = jnp.where(open_keys, 0.0, -jnp.inf).astype(F32)
        bias_ref[lo : lo + WIN, :] = row
        bias_ref[tok + lo : tok + lo + WIN, :] = row
    for load in loads[:3]:
        load.wait()
    noise = noise_ref[...]
    gain_ref[...] = 1.0 + jnp.dot(
        noise, w_gamma_ref[...], precision=lax.Precision.HIGHEST, preferred_element_type=F32
    )
    shift_ref[...] = jnp.dot(
        noise, w_beta_ref[...], precision=lax.Precision.HIGHEST, preferred_element_type=F32
    )
    encode(0, grid_ref[...], enc_ref[...], my_space * grid_dev)
    pl.semaphore_wait(barrier, plane - 1 + n_dp - 1)

    side_copies = []
    for slot, step in ((0, 1), (1, n_space - 1)):
        target = {"space": lax.rem(my_space + step, n_space)}
        side_copies.append(
            send(grid_ref, side_grid.at[slot], side_s.at[2 * slot], side_r.at[2 * slot], target)
        )
        side_copies.append(
            send(enc_ref, side_enc.at[slot], side_s.at[2 * slot + 1], side_r.at[2 * slot + 1], target)
        )

    for load in loads[3:]:
        load.wait()
    members = [slice(m, m + 1) for m in range(mine)]
    for m in members:
        inputs_ref[m.start * tok : m.stop * tok, :] = (
            normed_ref[:tok, :] * gain_ref[m, :] + shift_ref[m, :]
        ).astype(BF16)

    def columns(chunk):
        return pl.ds(pl.multiple_of(chunk * CHUNK, CHUNK), CHUNK)

    def project_queries(chunk, carry):
        out = jnp.dot(
            inputs_ref[: mine * tok, :], w_qkv_ref[:, columns(chunk)], preferred_element_type=F32
        ).astype(BF16)
        q_ref[:, :, columns(chunk)] = out.reshape(mine, tok, CHUNK)
        return carry

    def project_keys(lo, hi):
        def step(chunk, carry):
            out = jnp.dot(
                inputs_ref[: mine * (hi - lo), :],
                w_qkv_ref[:, columns(chunk + d_model // CHUNK)],
                preferred_element_type=F32,
            ).astype(BF16)
            kv_ref[:, lo:hi, columns(chunk)] = out.reshape(mine, hi - lo, CHUNK)
            return carry

        lax.fori_loop(0, 2 * d_model // CHUNK, step, 0)

    lax.fori_loop(0, d_model // CHUNK, project_queries, 0)
    project_keys(0, tok)
    for copy in side_copies:
        copy.wait()
    encode(1, side_grid[0], side_enc[0], lax.rem(my_space + n_space - 1, n_space) * grid_dev)
    encode(2, side_grid[1], side_enc[1], lax.rem(my_space + 1, n_space) * grid_dev)
    for m in members:
        inputs_ref[m.start * 2 * tok : m.stop * 2 * tok, :] = (
            normed_ref[tok:, :] * gain_ref[m, :] + shift_ref[m, :]
        ).astype(BF16)
    project_keys(tok, 3 * tok)

    def pred_copy(m, step):
        slot = m * (n_member - 1) + step - 1
        target = {"member": lax.rem(my_member + step, n_member)}
        return remote(
            pred_ref.at[m], others_ref.at[step - 1, m], pred_s.at[slot], pred_r.at[slot], target
        )

    pair_lane = lax.broadcasted_iota(jnp.int32, (tok, 2 * HD), 1)
    first = jnp.where(pair_lane < HD, HD ** (-0.5), 0.0).astype(BF16)
    second = jnp.where(pair_lane < HD, 0.0, HD ** (-0.5)).astype(BF16)

    def one_member(m, carry):
        for pair in range(d_model // (2 * HD)):
            cols = slice(pair * 2 * HD, (pair + 1) * 2 * HD)
            q = q_ref[m, :, cols]
            both = jnp.concatenate([q * first, q * second], axis=0)
            scores = lax.dot_general(both, kv_ref[m, :, cols], NT, preferred_element_type=F32)
            scores = scores + bias_ref[...]
            e = jnp.exp(scores - jnp.max(scores, axis=-1, keepdims=True))
            weights = (e * (1.0 / jnp.sum(e, axis=-1, keepdims=True))).astype(BF16)
            v = kv_ref[m, :, d_model + pair * 2 * HD : d_model + (pair + 1) * 2 * HD]
            out = jnp.dot(weights, v, preferred_element_type=F32)
            att_ref[:, cols] = jnp.where(pair_lane < HD, out[:tok], out[tok:]).astype(BF16)
        updated = states_ref[...] + jnp.dot(att_ref[...], w_o_ref[...], preferred_element_type=F32)
        dec_counts = dec_counts_ref[...]
        features = (
            jnp.dot(
                jnp.concatenate([dec_counts] * 3, axis=1),
                jnp.concatenate(parts(updated), axis=0),
                preferred_element_type=F32,
            )
            * (1.0 / k_dec)
        ).astype(BF16)
        feat_ref[m] = features
        pred_ref[m] = (
            grid_ref[...].astype(F32)
            + lax.dot_general(readout_ref[...], features, NT, preferred_element_type=F32)
        ).astype(BF16)
        for step in range(1, n_member):
            pred_copy(m, step).start()
        return carry

    lax.fori_loop(0, mine, one_member, 0)

    def resident(n):
        if n < mine:
            return pred_ref[n].astype(F32)
        return others_ref[n // mine - 1, n % mine].astype(F32)

    def squares(left, right):
        gap = left - right
        line = jnp.sum(gap * gap, axis=0, keepdims=True)
        total = line[:, :128]
        for lane in range(128, grid_dev, 128):
            total = total + line[:, lane : lane + 128]
        return total

    dist_ref[my_space] = jnp.zeros(dist_ref.shape[1:], F32)
    truth = target_ref[...].astype(F32)
    for m in range(mine):
        x = resident(m)
        dist_ref[my_space, pair_rows + m : pair_rows + m + 1, :] = squares(x, truth)
        for n in range(m + 1, mine):
            line = squares(x, resident(n))
            for row in (m * everyone + n, n * everyone + m):
                dist_ref[my_space, row : row + 1, :] = line
    for other in range(mine):
        for step in range(1, n_member):
            pred_copy(other, step).wait()
            n = step * mine + other
            y = resident(n)
            for m in range(mine):
                row = m * everyone + n
                dist_ref[my_space, row : row + 1, :] = squares(resident(m), y)
    copies = []
    for step in range(1, n_space):
        target = {"space": lax.rem(my_space + step, n_space)}
        copies.append(
            send(dist_ref.at[my_space], dist_ref.at[my_space], dist_s.at[step - 1], dist_r.at[step - 1], target)
        )
    for copy in copies:
        copy.wait()
    total = dist_ref[0]
    for s in range(1, n_space):
        total = total + dist_ref[s]
    dist = jnp.sqrt(jnp.sum(total, axis=-1, keepdims=True) + EPSILON)
    pull = 1.0 / dist
    row_id = lax.broadcasted_iota(jnp.int32, dist.shape, 0)
    share = jnp.where(row_id < pair_rows, -1.0 / (2.0 * everyone * everyone), 1.0 / everyone)
    share = jnp.where(row_id >= pair_rows + mine, 0.0, share)
    for m in range(mine):
        share = jnp.where(row_id == m * everyone + m, 0.0, share)
    score = jnp.sum(dist * share, axis=0, keepdims=True)
    score_m[my_member] = jnp.broadcast_to(score, score_m.shape[1:])
    copies = []
    for step in range(1, n_member):
        target = {"member": lax.rem(my_member + step, n_member)}
        copies.append(
            send(score_m.at[my_member], score_m.at[my_member], sm_s.at[step - 1], sm_r.at[step - 1], target)
        )
    grad = jnp.zeros((v_count, feat_ref.shape[2]), F32)
    for m in range(mine):
        x = resident(m)
        truth_pull = pull[pair_rows + m : pair_rows + m + 1, :] * (1.0 / everyone)
        slope = truth_pull * (x - truth)
        own_pull = jnp.zeros((1, 1), F32)
        mixed = jnp.zeros_like(x)
        for n in range(everyone):
            if n != m:
                row = m * everyone + n
                b = pull[row : row + 1, :] * (1.0 / (everyone * everyone))
                own_pull = own_pull + b
                mixed = mixed + b * resident(n)
        slope = (slope - own_pull * x + mixed).astype(BF16)
        grad = grad + jnp.dot(slope, feat_ref[m], preferred_element_type=F32)
    grad_ref[v_count:, :] = jnp.zeros((grad_ref.shape[0] - v_count, grad_ref.shape[1]), F32)
    grad_ref[:v_count, :] = grad
    for owner in range(plane):
        share_out[owner] = grad_ref[owner * rows : (owner + 1) * rows, :].astype(BF16)
    share_copies = []
    for step in range(1, plane):
        peer, target = plane_peer(step)
        share_copies.append(
            send(share_out.at[peer], share_in.at[me], share_s.at[step - 1], share_r.at[step - 1], target)
        )
    share_in[me] = share_out[me]
    for copy in copies:
        copy.wait()
    total = score_m[0]
    for s in range(1, n_member):
        total = total + score_m[s]
    score_d[my_dp] = total
    copies = []
    for step in range(1, n_dp):
        target = {"dp": lax.rem(my_dp + step, n_dp)}
        copies.append(
            send(score_d.at[my_dp], score_d.at[my_dp], sd_s.at[step - 1], sd_r.at[step - 1], target)
        )
    for copy in share_copies:
        copy.wait()
    total = share_in[0].astype(F32)
    for s in range(1, plane):
        total = total + share_in[s].astype(F32)
    mid_in[my_dp] = total.astype(BF16)
    mid_copies = []
    for step in range(1, n_dp):
        target = {"dp": lax.rem(my_dp + step, n_dp)}
        mid_copies.append(
            send(mid_in.at[my_dp], mid_in.at[my_dp], mid_s.at[step - 1], mid_r.at[step - 1], target)
        )
    for copy in copies:
        copy.wait()
    total = score_d[0]
    for s in range(1, n_dp):
        total = total + score_d[s]
    grid_total = grid_dev * n_space
    total = total / (n_dp * jnp.sqrt(jnp.full(total.shape, float(v_count * grid_total), F32)))
    score_ref[0, 0] = jnp.max(total)
    for copy in mid_copies:
        copy.wait()
    total = mid_in[0].astype(F32)
    for s in range(1, n_dp):
        total = total + mid_in[s].astype(F32)
    full_ref[me] = total.astype(BF16)
    copies = []
    for step in range(1, plane):
        copies.append(
            send(full_ref.at[me], full_ref.at[me], full_s.at[step - 1], full_r.at[step - 1], plane_peer(step)[1])
        )
    for copy in copies:
        copy.wait()
    square = jnp.zeros((1, full_ref.shape[2]), F32)
    for owner in range(plane):
        piece = full_ref[owner].astype(F32)
        square = square + jnp.sum(piece * piece, axis=0, keepdims=True)
    square = jnp.sum(square, axis=-1, keepdims=True)
    scale = 1.0 / jnp.sqrt(square / (v_count * full_ref.shape[2]) + EPSILON)
    for owner in range(plane):
        keep = min(rows, v_count - owner * rows)
        if keep > 0:
            slope_out_ref[owner * rows : owner * rows + keep, :] = full_ref[owner].astype(F32)[:keep, :] * scale


def solution(mesh):
    sizes = tuple(mesh.shape[name] for name in ("dp", "member", "space"))
    n_dp, n_member, n_space = sizes
    plane = n_member * n_space

    def body(
        grid_in, target, noise, neighbours, enc_index, dec_index,
        w_in, w_gamma, w_beta, w_qkv, w_o, readout_matrix,
    ):
        v_count, grid_dev = target.shape[1:]
        mine = noise.shape[1]
        d_model = w_o.shape[0]
        tok = enc_index.shape[0]
        rows = -(-v_count // plane)
        dist_rows = -(-(mine * mine * n_member + mine) // 8) * 8
        grad_rows = max(plane * rows, v_count + 1)
        whole = pl.BlockSpec(memory_space=pltpu.VMEM)
        smem = pl.BlockSpec(memory_space=pltpu.SMEM)
        away = pl.BlockSpec(memory_space=pl.ANY)

        def sems(count):
            return [pltpu.SemaphoreType.DMA((count,))] * 2

        loaded = (target[0], w_in, w_gamma, w_beta, w_qkv, w_o, readout_matrix)
        pred, score, slope = pl.pallas_call(
            functools.partial(window_kernel, sizes),
            out_shape=(
                jax.ShapeDtypeStruct((mine, v_count, grid_dev), BF16),
                jax.ShapeDtypeStruct((1, 1), F32),
                jax.ShapeDtypeStruct((v_count, d_model), F32),
            ),
            in_specs=[smem] + [whole] * 4 + [away] * len(loaded),
            out_specs=(whole, smem, whole),
            scratch_shapes=[pltpu.VMEM(x.shape, x.dtype) for x in loaded]
            + [
                pltpu.SemaphoreType.DMA((len(loaded),)),
                pltpu.VMEM((2, v_count, grid_dev), BF16),
                pltpu.VMEM((2,) + enc_index.shape[::-1], jnp.int32),
            ]
            + sems(4)
            + [
                pltpu.VMEM((tok, d_model), F32),
                pltpu.VMEM((3 * tok, d_model), F32),
                pltpu.VMEM((mine, d_model), F32),
                pltpu.VMEM((mine, d_model), F32),
                pltpu.VMEM((grid_dev, tok), BF16),
                pltpu.VMEM((2 * tok, 3 * tok), F32),
                pltpu.VMEM((mine * 2 * tok, d_model), BF16),
                pltpu.VMEM((mine, tok, d_model), BF16),
                pltpu.VMEM((mine, 3 * tok, 2 * d_model), BF16),
                pltpu.VMEM((tok, d_model), BF16),
                pltpu.VMEM((mine, grid_dev, d_model), BF16),
                pltpu.VMEM((n_member - 1, mine, v_count, grid_dev), BF16),
                pltpu.VMEM((n_space, dist_rows, 128), F32),
                pltpu.VMEM((grad_rows, d_model), F32),
                pltpu.VMEM((plane, rows, d_model), BF16),
                pltpu.VMEM((plane, rows, d_model), BF16),
                pltpu.VMEM((n_dp, rows, d_model), BF16),
                pltpu.VMEM((plane, rows, d_model), BF16),
                pltpu.VMEM((n_member, 8, 128), F32),
                pltpu.VMEM((n_dp, 8, 128), F32),
            ]
            + sems((n_member - 1) * mine) + sems(n_space - 1) + sems(plane - 1) + sems(n_dp - 1)
            + sems(plane - 1) + sems(n_member - 1) + sems(n_dp - 1),
            compiler_params=pltpu.CompilerParams(
                collective_id=0, has_side_effects=True, vmem_limit_bytes=VMEM_LIMIT
            ),
            name="training_window",
        )(
            neighbours, grid_in[0], enc_index.T, dec_index.T, noise[0], *loaded
        )
        return (pred[None], score[0, 0], slope)

    in_specs = (
        P("dp", None, "space"),
        P("dp", None, "space"),
        P("dp", "member", None),
        P("space", None),
        P("space", None),
        P("space", None),
        P(),
        P(),
        P(),
        P(),
        P(),
        P(),
    )
    out_specs = (P("dp", "member", None, "space"), P(), P())
    return jax.shard_map(body, mesh=mesh, in_specs=in_specs, out_specs=out_specs, check_vma=False)
```
